128 devices in a mesh: pool: 16 (over y, x), tensor: 8 (over z, core).
Axes of the slice: x: 4, y: 4, z: 4, core: 2. Of those that a mesh axis runs over, the one named last changes fastest.
Arguments:
- inputs: bfloat16 [1024, 8192], P(None, 'pool'), may hold values from -160 to 160
- attn_gain: bfloat16 [8192], P('pool'), may hold values from 0.5 to 1.5
- query_key_value_weight: bfloat16 [8192, 10240], P('pool', 'tensor'), may hold values from -0.0625 to 0.0625
- key_value_pages: bfloat16 [1024, 128, 8, 256], P('pool', None, 'tensor'), may hold values from -210 to 210, as said below
- w_out: bfloat16 [8192, 8192], P('tensor', 'pool'), may hold values from -0.5 to 0.5
- ffn_gain: bfloat16 [8192], P('pool'), may hold values from 0.5 to 1.5
- w_gate_up: bfloat16 [8192, 2, 28672], P('pool', None, 'tensor'), may hold values from -0.0625 to 0.0625
- w_down: bfloat16 [28672, 8192], P('tensor', 'pool'), may hold values from -0.0625 to 0.0625
- owner_pool_device: int32 [1024], replicated, may hold values from 0 to 15, as said below
- context_page_count: int32 [1024], replicated, may hold values from 1 to 8, as said below
- request_page_slots: int32 [1024, 8], replicated, may hold values from 0 to 63
- mig_page: int32 [16, 16], P('pool'), may hold values from 0 to 63
- mig_dest: int32 [16, 16], P('pool'), may hold values from 0 to 15, as said below
- mig_slot: int32 [16, 16], P('pool'), may hold values from 0 to 63, as said below
Outputs:
- out_rows: bfloat16 [1024, 8192], P(None, 'pool')
- new_pool: bfloat16 [1024, 128, 8, 256], P('pool', None, 'tensor')
The draws below stay inside these ranges and needn't reach their ends.
Inputs may be any that keep to these rules, and one draw needn't show every extreme that they name: `key_value_pages`: cached keys (first 128 entries of the last dimension, rotary embedding already applied) and values (last 128). `owner_pool_device`: each aligned block of 64 requests names every pool device at most 8 times, and in every block one pool device is named exactly 8 times. `context_page_count`: at least one request has exactly 8 pages. `request_page_slots`: entries at or beyond a request's page count are not used. `mig_dest`: no row names one destination more than 2 times, and every row names one exactly 2 times. `mig_slot`: no two moved pages take the same slot of the same destination.
All inputs are finite; a program needn't handle non-finite values.
Results may differ from the reference program's by a relative error of at most 0.013.
Values may be sent and summed in bfloat16 or wider, within the bound.
No kernel may reach another device: no remote copies, remote signals or barrier semaphores. Data moves between devices by JAX's collectives and lax.ppermute only.
A program may use at most 192 MiB of HBM per device.

```python
import math
import jax
import jax.numpy as jnp
from jax import lax

MODEL_WIDTH = 8192
QUERY_HEADS = 64
KEY_VALUE_HEADS = 8
HEAD_SIZE = 128
FF = 28672
REQ_DEV = 64
POOL_PAGE_SLOTS = 64
PAGE_TOKENS = 128
MAX_CONTEXT_PAGE = 8
MCAP = 2
REQUESTS = 1024
CAP = 8
MIG = 16
N_POOL = 16


def draw_inputs(key, part):
    first_key, second_key = jax.random.split(key)
    columns = jnp.arange(MODEL_WIDTH, dtype=jnp.float32) / MODEL_WIDTH
    values = jnp.clip(jax.random.normal(first_key, (REQUESTS, MODEL_WIDTH), jnp.float32), -4.0, 4.0)
    col_scale = 3.0 ** columns
    row_scale = jnp.exp(jax.random.uniform(second_key, (REQUESTS, 1), jnp.float32, math.log(0.5), math.log(2.0)))
    return (values * col_scale[None, :] * row_scale).astype(jnp.bfloat16)


def draw_key_value_pages(key, part):
    first_key = jax.random.fold_in(key, 0)
    array_shape = (N_POOL * POOL_PAGE_SLOTS, PAGE_TOKENS, KEY_VALUE_HEADS, 2 * HEAD_SIZE)
    result = jnp.clip(jax.random.normal(first_key, array_shape, jnp.float32), -4.0, 4.0)
    return result.astype(jnp.bfloat16)


def draw_owner_pool_device(key, part):
    hot_owner = jax.random.randint(jax.random.fold_in(key, 11), (), 0, N_POOL)

    def one_block(number):
        sub_key = jax.random.fold_in(key, 100 + number)
        pick_key, order_key = jax.random.split(sub_key)
        picks = jax.random.permutation(pick_key, (N_POOL - 1) * CAP)[:REQ_DEV - CAP]
        others = (hot_owner + 1 + picks // CAP) % N_POOL
        owners = jnp.concatenate([jnp.full((CAP,), hot_owner, jnp.int32), others.astype(jnp.int32)])
        return jax.random.permutation(order_key, owners)
    return jax.vmap(one_block)(jnp.arange(N_POOL, dtype=jnp.int32)).reshape(-1).astype(jnp.int32)


def draw_context_page_count(key, part):
    first_key, second_key = jax.random.split(key)
    lengths = jax.random.randint(first_key, (REQUESTS,), 1, MAX_CONTEXT_PAGE + 1)
    chosen = jax.random.randint(second_key, (), 0, REQUESTS)
    return jnp.where(jnp.arange(REQUESTS) == chosen, MAX_CONTEXT_PAGE, lengths).astype(jnp.int32)


def move_plan(key):
    base_key = jax.random.fold_in(key, 23)

    def slot_row(target):
        return jax.random.permutation(jax.random.fold_in(base_key, 1000 + target), POOL_PAGE_SLOTS)[:N_POOL * MCAP]
    slot_tables = jax.vmap(slot_row)(jnp.arange(N_POOL, dtype=jnp.int32))

    def one_source(source):
        order_key, pick_key, shuffle_key = jax.random.split(jax.random.fold_in(base_key, source), 3)
        order = jax.random.permutation(order_key, N_POOL)
        picks = jax.random.permutation(pick_key, (N_POOL - 1) * MCAP)[:MIG - MCAP]
        targets = jnp.concatenate([jnp.full((MCAP,), order[0]), order[1 + picks // MCAP]])
        ranks = jnp.concatenate([jnp.arange(MCAP), picks % MCAP])
        shuffle = jax.random.permutation(shuffle_key, MIG)
        targets = targets[shuffle]
        ranks = ranks[shuffle]
        slots = slot_tables[targets, source * MCAP + ranks]
        return (targets.astype(jnp.int32), slots.astype(jnp.int32))
    return jax.vmap(one_source)(jnp.arange(N_POOL, dtype=jnp.int32))


def draw_mig_dest(key, part):
    return move_plan(key)[0]


def draw_mig_slot(key, part):
    return move_plan(key)[1]


def place_ends(values, key, low, high):
    longest = values.shape.index(max(values.shape))
    spots = []
    for shift in (0, 1):
        where = [jax.random.randint(jax.random.fold_in(key, axis), (), 0, length) for axis, length in enumerate(values.shape)]
        where[longest] = (where[longest] + shift) % values.shape[longest]
        spots.append(tuple(where))
    return values.at[spots[0]].set(low).at[spots[1]].set(high)


def block_scale(key, extent, pieces, low, largest):
    factor_of, own = 1.0, jax.random.fold_in(key, 6)
    for axis_at, blocks in pieces:
        steps = jnp.exp(jax.random.uniform(jax.random.fold_in(own, axis_at), (blocks,), jnp.float32, low / len(pieces), largest / len(pieces)))
        factor_of = factor_of * jnp.repeat(steps, extent[axis_at] // blocks).reshape([-1 if axis == axis_at else 1 for axis in range(len(extent))])
    return factor_of


def gaussian(rng, shape, deviation, most, pieces=(), kind=jnp.bfloat16):
    drawn = deviation * jax.random.normal(rng, shape, jnp.float32)
    if pieces:
        drawn = drawn * block_scale(rng, shape, pieces, -0.22, 0.18)
    return jnp.clip(drawn, -most, most).astype(kind)


def setup_inputs(seed: int = 0) -> dict:
    arg_keys = jax.random.split(jax.random.key(seed), 15)
    inputs = draw_inputs(jax.random.fold_in(arg_keys[14], 71), 0)
    attn_gain = jnp.clip(1.0 + 0.1 * jax.random.normal(arg_keys[1], (MODEL_WIDTH,), jnp.float32), 0.5, 1.5).astype(jnp.bfloat16)
    query_key_value_weight = gaussian(arg_keys[2], (MODEL_WIDTH, (QUERY_HEADS + 2 * KEY_VALUE_HEADS) * HEAD_SIZE), MODEL_WIDTH ** -0.5, 0.0625, ((0, 16), (1, 8)))
    key_value_pages = draw_key_value_pages(jax.random.fold_in(arg_keys[14], 71), 0)
    w_out = gaussian(arg_keys[4], (QUERY_HEADS * HEAD_SIZE, MODEL_WIDTH), (QUERY_HEADS * HEAD_SIZE // 64) ** -0.5, 0.5, ((0, 8), (1, 16)))
    ffn_gain = jnp.clip(1.0 + 0.1 * jax.random.normal(arg_keys[5], (MODEL_WIDTH,), jnp.float32), 0.5, 1.5).astype(jnp.bfloat16)
    w_gate_up = gaussian(arg_keys[6], (MODEL_WIDTH, 2, FF), MODEL_WIDTH ** -0.5, 0.0625, ((0, 16), (2, 8)))
    w_down = gaussian(arg_keys[7], (FF, MODEL_WIDTH), (FF // 4) ** -0.5, 0.0625, ((0, 8), (1, 16)))
    owner_pool_device = draw_owner_pool_device(jax.random.fold_in(arg_keys[14], 71), 0)
    context_page_count = draw_context_page_count(jax.random.fold_in(arg_keys[14], 71), 0)
    request_page_slots = place_ends(jax.random.randint(arg_keys[10], (REQUESTS, MAX_CONTEXT_PAGE), 0, POOL_PAGE_SLOTS), jax.random.fold_in(arg_keys[10], 1), 0, POOL_PAGE_SLOTS - 1).astype(jnp.int32)
    mig_page = place_ends(jax.random.randint(arg_keys[11], (N_POOL, MIG), 0, POOL_PAGE_SLOTS), jax.random.fold_in(arg_keys[11], 1), 0, POOL_PAGE_SLOTS - 1).astype(jnp.int32)
    mig_dest = draw_mig_dest(jax.random.fold_in(arg_keys[14], 71), 0)
    mig_slot = draw_mig_slot(jax.random.fold_in(arg_keys[14], 71), 0)
    return dict(inputs=inputs, attn_gain=attn_gain, query_key_value_weight=query_key_value_weight, key_value_pages=key_value_pages, w_out=w_out, ffn_gain=ffn_gain, w_gate_up=w_gate_up, w_down=w_down, owner_pool_device=owner_pool_device, context_page_count=context_page_count, request_page_slots=request_page_slots, mig_page=mig_page, mig_dest=mig_dest, mig_slot=mig_slot)


epsilon = 1e-05

def rotate_halves(vectors, token_positions):
    half_dim = vectors.shape[-1] // 2
    steps_index = jnp.arange(half_dim, dtype=jnp.float32)
    frequency = jnp.exp(steps_index * (-2.0 * math.log(500000.0) / vectors.shape[-1]))
    angles = token_positions.astype(jnp.float32)[:, None] * frequency[None, :]
    cosine = jnp.cos(angles)[:, None, :]
    sine_part = jnp.sin(angles)[:, None, :]
    front_half = vectors[..., :half_dim]
    back_half = vectors[..., half_dim:]
    return jnp.concatenate([front_half * cosine - back_half * sine_part, back_half * cosine + front_half * sine_part], axis=-1)

def reference(inputs, attn_gain, query_key_value_weight, key_value_pages, w_out, ffn_gain, w_gate_up, w_down, owner_pool_device, context_page_count, request_page_slots, mig_page, mig_dest, mig_slot):
    request_total = inputs.shape[0]
    query_groups = QUERY_HEADS // KEY_VALUE_HEADS
    residual = inputs.astype(jnp.float32)
    mean_square = lax.optimization_barrier(jnp.mean(residual * residual, axis=1, keepdims=True))
    normed_input = (residual * lax.rsqrt(mean_square + epsilon) * attn_gain.astype(jnp.float32)).astype(jnp.bfloat16)
    project_input = jnp.dot(normed_input, query_key_value_weight, preferred_element_type=jnp.float32).reshape(request_total, KEY_VALUE_HEADS, query_groups + 2, HEAD_SIZE)
    token_positions = context_page_count * PAGE_TOKENS
    query_rows = rotate_halves(project_input[:, :, :query_groups].reshape(request_total, QUERY_HEADS, HEAD_SIZE), token_positions).astype(jnp.bfloat16).reshape(request_total, KEY_VALUE_HEADS, query_groups, HEAD_SIZE)
    fresh_keys = rotate_halves(project_input[:, :, query_groups], token_positions).astype(jnp.bfloat16)
    fresh_values = project_input[:, :, query_groups + 1].astype(jnp.bfloat16)
    context_span = MAX_CONTEXT_PAGE * PAGE_TOKENS
    scale = 1.0 / math.sqrt(HEAD_SIZE)

    def attend_pages(blocks):
        query, own_key, own_val, owners, lengths, table = blocks
        item_count = query.shape[0]
        page_token_rows = owners[:, None] * POOL_PAGE_SLOTS + table
        gathered_pages = key_value_pages[page_token_rows].reshape(item_count, context_span, KEY_VALUE_HEADS, 2 * HEAD_SIZE)
        keys = gathered_pages[..., :HEAD_SIZE].astype(jnp.float32)
        values = gathered_pages[..., HEAD_SIZE:].astype(jnp.float32)
        query_f = query.astype(jnp.float32)
        scores = jnp.einsum('nhgd,nthd->nhgt', query_f, keys) * scale
        valid = (jnp.arange(context_span)[None, :] < (lengths * PAGE_TOKENS)[:, None])[:, None, None, :]
        scores = jnp.where(valid, scores, -1e+30)
        self_score = jnp.einsum('nhgd,nhd->nhg', query_f, own_key.astype(jnp.float32)) * scale
        top = jnp.maximum(lax.optimization_barrier(jnp.max(scores, axis=-1)), self_score)
        expo = jnp.where(valid, jnp.exp(scores - top[..., None]), 0.0)
        self_exp = jnp.exp(self_score - top)
        total = lax.optimization_barrier(jnp.sum(expo, axis=-1)) + self_exp
        weights = (expo / total[..., None]).astype(jnp.bfloat16)
        self_weight = (self_exp / total).astype(jnp.bfloat16)
        mixed = jnp.einsum('nhgt,nthd->nhgd', weights.astype(jnp.float32), values)
        mixed = mixed + self_weight.astype(jnp.float32)[..., None] * own_val.astype(jnp.float32)[:, :, None, :]
        return mixed.astype(jnp.bfloat16).reshape(item_count, QUERY_HEADS * HEAD_SIZE)
    column_width = 8
    while request_total % column_width:
        column_width = column_width // 2
    block_total = request_total // column_width
    attention_output = lax.map(attend_pages, (query_rows.reshape(block_total, column_width, KEY_VALUE_HEADS, query_groups, HEAD_SIZE), fresh_keys.reshape(block_total, column_width, KEY_VALUE_HEADS, HEAD_SIZE), fresh_values.reshape(block_total, column_width, KEY_VALUE_HEADS, HEAD_SIZE), owner_pool_device.reshape(block_total, column_width), context_page_count.reshape(block_total, column_width), request_page_slots.reshape(block_total, column_width, MAX_CONTEXT_PAGE)))
    attention_output = attention_output.reshape(request_total, QUERY_HEADS * HEAD_SIZE)
    middle = residual + jnp.dot(attention_output, w_out, preferred_element_type=jnp.float32)
    mid_square = lax.optimization_barrier(jnp.mean(middle * middle, axis=1, keepdims=True))
    ffn_in = (middle * lax.rsqrt(mid_square + epsilon) * ffn_gain.astype(jnp.float32)).astype(jnp.bfloat16)
    gate_up = jnp.dot(ffn_in, w_gate_up.reshape(MODEL_WIDTH, 2 * FF), preferred_element_type=jnp.float32)
    hidden = (jax.nn.silu(gate_up[:, :FF]) * gate_up[:, FF:]).astype(jnp.bfloat16)
    out_rows = (middle + jnp.dot(hidden, w_down, preferred_element_type=jnp.float32)).astype(jnp.bfloat16)
    source_rows = (jnp.arange(N_POOL, dtype=jnp.int32)[:, None] * POOL_PAGE_SLOTS + mig_page).reshape(-1)
    target_rows = (mig_dest * POOL_PAGE_SLOTS + mig_slot).reshape(-1)
    new_pool = key_value_pages.at[target_rows].set(key_value_pages[source_rows])
    return (out_rows, new_pool)
```

```python
import functools
import math

import jax
import jax.numpy as jnp
from jax import lax
from jax.experimental import pallas as pl
from jax.experimental.pallas import tpu as pltpu
from jax.sharding import Mesh
from jax.sharding import PartitionSpec as P

MCAP = 2
EPS = 1e-05
F32 = jnp.float32
BF16 = jnp.bfloat16
POOL = ("y", "x")
SIDE = 4
VMEM_SPEC = pl.BlockSpec(memory_space=pltpu.VMEM)


def shift(v, axis, s):
    return lax.ppermute(v, axis, [(i, (i + s) % SIDE) for i in range(SIDE)])


def swap(v):
    return lax.ppermute(v, "c", [(0, 1), (1, 0)])


def pick(v, index, axis=0):
    return lax.dynamic_index_in_dim(v, index, axis, keepdims=False)


def reduce_four(get, axis, here):
    got = {}
    for s in (2, 1, 3):
        got[s] = shift(get((here + s) % SIDE), axis, s)
    total = get(here).astype(F32)
    for s in (2, 1, 3):
        total = total + got[s].astype(F32)
    return total


def gather_direct(v, axis):
    got = {s: shift(v, axis, s) for s in (2, 1, 3)}
    return [v, got[1], got[2], got[3]]


def gather_ring(v, axis):
    half = v.shape[0] // 2
    fwd = shift(v, axis, 1)
    bwd = shift(v, axis, 3)
    far_a = shift(fwd[:half], axis, 1)
    far_b = shift(bwd[half:], axis, 3)
    return [v, fwd, (far_a, far_b), bwd]


def place(blocks, here):
    buf = jnp.zeros((SIDE,) + blocks[0].shape, blocks[0].dtype)
    for s in range(SIDE):
        buf = lax.dynamic_update_index_in_dim(buf, blocks[s], (here - s) % SIDE, 0)
    return buf


def three_parts(v):
    high = lax.reduce_precision(v, 8, 7)
    rest = v - high
    mid = lax.reduce_precision(rest, 8, 7)
    return high, mid, rest - mid


def attention_kernel(ids_ref, count_ref, slots_ref, q_ref, kv_ref, o_ref, *, scale, group, dim, most, last):
    page_len = kv_ref.shape[1]
    lane = lax.broadcasted_iota(jnp.int32, (8, most * page_len), 1)

    def body(step, carry):
        held = []
        for u in range(group):
            r = step * group + u
            rid = ids_ref[r]
            safe = jnp.minimum(rid, last)
            n = jnp.where(rid > last, 0, count_ref[safe])
            pages = [slots_ref[j, safe] for j in range(most)]
            qkv = q_ref[r]
            q = qkv[:8]
            keys = jnp.concatenate([kv_ref[p, :, :dim] for p in pages], axis=0)
            s = lax.dot_general(q, keys, (((1,), (1,)), ((), ())), preferred_element_type=F32)
            held.append((r, pages, qkv, q, jnp.where(lane < n * page_len, s * scale, -1e30)))
        soft = []
        for r, pages, qkv, q, s in held:
            self_score = jnp.sum(q.astype(F32) * qkv[8:9].astype(F32), axis=1, keepdims=True) * scale
            top = jnp.maximum(jnp.max(s, axis=1, keepdims=True), self_score)
            expo = jnp.exp(s - top)
            self_exp = jnp.exp(self_score - top)
            total = jnp.sum(expo, axis=1, keepdims=True) + self_exp
            inverse = 1.0 / total
            own = (self_exp * inverse).astype(BF16).astype(F32) * qkv[9:10].astype(F32)
            soft.append(((expo * inverse).astype(BF16), own))
        for (r, pages, qkv, q, s), (w, own) in zip(held, soft):
            values = jnp.concatenate([kv_ref[p, :, dim:] for p in pages], axis=0)
            o_ref[r] = (jnp.dot(w, values, preferred_element_type=F32) + own).astype(BF16)
        return carry

    lax.fori_loop(0, q_ref.shape[0] // group, body, 0)


def attend(ids, counts, slots_t, q, kv):
    rows, parts, dim = q.shape
    kernel = functools.partial(
        attention_kernel,
        scale=1.0 / math.sqrt(dim),
        group=8,
        dim=dim,
        most=slots_t.shape[0],
        last=counts.shape[0] - 1,
    )
    smem = pl.BlockSpec(memory_space=pltpu.SMEM)
    return pl.pallas_call(
        kernel,
        out_shape=jax.ShapeDtypeStruct((rows, 8, dim), BF16),
        in_specs=[smem, smem, smem, VMEM_SPEC, VMEM_SPEC],
        out_specs=VMEM_SPEC,
        compiler_params=pltpu.CompilerParams(vmem_limit_bytes=32 << 20),
        cost_estimate=pl.CostEstimate(flops=600_000_000, bytes_accessed=6_000_000, transcendentals=1_000_000),
        name="paged_attention",
    )(ids, counts, slots_t, q, kv)


SMEM_SPEC = pl.BlockSpec(memory_space=pltpu.SMEM)


def split_terms(v):
    high = v.astype(BF16).astype(F32)
    mid = (v - high).astype(BF16).astype(F32)
    low = v - high - mid
    lane = lax.broadcasted_iota(jnp.int32, (v.shape[0], 128), 1)
    return jnp.where(lane == 0, high, jnp.where(lane == 1, mid, jnp.where(lane == 2, low, 0.0))).astype(BF16)


def qkv_kernel(x_ref, gain_ref, w_ref, out_ref):
    gain = gain_ref[...].astype(F32)
    cols = w_ref.shape[1]
    span = 256
    for k in range(x_ref.shape[0] // span):
        rows = slice(k * span, (k + 1) * span)
        wide = x_ref[rows, :].astype(F32)
        out_ref[rows, :cols] = jnp.dot(
            (wide * gain).astype(BF16), w_ref[...], preferred_element_type=F32
        ).astype(BF16)
        out_ref[rows, cols:] = split_terms(jnp.sum(wide * wide, axis=1, keepdims=True))


def qkv_product(inputs, gain, weight):
    rows, width = inputs.shape
    cols = weight.shape[1]
    return pl.pallas_call(
        qkv_kernel,
        out_shape=jax.ShapeDtypeStruct((rows, cols + 128), BF16),
        in_specs=[VMEM_SPEC] * 3,
        out_specs=VMEM_SPEC,
        compiler_params=pltpu.CompilerParams(vmem_limit_bytes=24 << 20),
        cost_estimate=pl.CostEstimate(flops=1_400_000_000, bytes_accessed=6_000_000, transcendentals=0),
        name="query_key_value",
    )(inputs, gain.reshape(1, -1), weight)


def ready_kernel(spread_ref, cos_ref, sin_ref, in_ref, out, rows, *, dim, full_width):
    def total(lo):
        acc = in_ref[0, :, lo : lo + 128].astype(F32)
        for t in range(1, in_ref.shape[0]):
            acc = acc + in_ref[t, :, lo : lo + 128].astype(F32)
        return acc

    cols = out.shape[1]
    scale = lax.rsqrt(jnp.sum(total(cols), axis=1, keepdims=True) / full_width + EPS)
    cos, sin = cos_ref[...], sin_ref[...]
    for h in range(cols // dim):
        lo = h * dim
        piece = total(lo) * scale
        if lo < cols - dim:
            piece = piece * cos + pltpu.roll(piece, dim // 2, 1) * sin
        rows[:, lo : lo + dim] = piece.astype(BF16)
    out[...] = jnp.dot(spread_ref[...], rows[...], preferred_element_type=F32).astype(BF16)


def ready_rows(spread, cos, sin, blocks, dim, full_width):
    slots, count = spread.shape
    cols = blocks.shape[2] - 128
    return pl.pallas_call(
        functools.partial(ready_kernel, dim=dim, full_width=full_width),
        out_shape=jax.ShapeDtypeStruct((slots, cols), BF16),
        in_specs=[VMEM_SPEC] * 4,
        out_specs=VMEM_SPEC,
        scratch_shapes=[pltpu.VMEM((count, cols), BF16)],
        cost_estimate=pl.CostEstimate(flops=30_000_000, bytes_accessed=3_500_000, transcendentals=0),
        name="ready_rows",
    )(spread, cos, sin, blocks)


def regroup_kernel(at_ref, w_ref, *refs, unit_a, unit_b):
    outs_a, outs_b = refs[:4], refs[4:8]
    base = SIDE * unit_a
    for s in range(SIDE):
        for out, first, unit, here in (
            (outs_a[s], 0, unit_a, at_ref[0]),
            (outs_b[s], base, unit_b, at_ref[1]),
        ):
            cols = pl.ds(pl.multiple_of(first + lax.rem(here + s, SIDE) * unit, 128), unit)
            pair = jnp.swapaxes(w_ref[:, :, cols], 0, 1)
            for j in range(unit // 128):
                for g in range(2):
                    lo = (2 * j + g) * 128
                    out[:, lo : lo + 128] = pair[g, :, j * 128 : (j + 1) * 128]


def regroup(at, weight, unit_a, unit_b):
    rows = weight.shape[0]
    step = 64
    outs = pl.pallas_call(
        functools.partial(regroup_kernel, unit_a=unit_a, unit_b=unit_b),
        out_shape=[jax.ShapeDtypeStruct((rows, 2 * unit_a), BF16)] * 4
        + [jax.ShapeDtypeStruct((rows, 2 * unit_b), BF16)] * 4,
        grid=(rows // step,),
        in_specs=[SMEM_SPEC, pl.BlockSpec((step,) + weight.shape[1:], lambda i: (i, 0, 0))],
        out_specs=[pl.BlockSpec((step, 2 * unit_a), lambda i: (i, 0))] * 4
        + [pl.BlockSpec((step, 2 * unit_b), lambda i: (i, 0))] * 4,
        compiler_params=pltpu.CompilerParams(vmem_limit_bytes=16 << 20),
        cost_estimate=pl.CostEstimate(flops=0, bytes_accessed=15_000_000, transcendentals=0),
        name="regroup_weights",
    )(at, weight)
    return outs[:4], outs[4:]


def term_rows(v):
    high = v.astype(BF16).astype(F32)
    mid = (v - high).astype(BF16).astype(F32)
    low = v - high - mid
    row = lax.broadcasted_iota(jnp.int32, (16, v.shape[1]), 0)
    return jnp.where(row == 0, high, jnp.where(row == 1, mid, jnp.where(row == 2, low, 0.0))).astype(BF16)


def hidden_kernel(*refs, full_width):
    ins, out = refs[:4], refs[4]
    rows = out.shape[1]
    diagonal = lax.broadcasted_iota(jnp.int32, (rows, rows), 0) == lax.broadcasted_iota(
        jnp.int32, (rows, rows), 1
    )
    for part in range(2):
        at = slice(part * rows, (part + 1) * rows)
        terms = ins[0][2 * rows :, at].astype(F32)
        for s in range(1, SIDE):
            terms = terms + ins[s][2 * rows :, at].astype(F32)
        squares = jnp.sum(terms, axis=0, keepdims=True)
        column = jnp.sum(jnp.where(diagonal, squares, 0.0), axis=1, keepdims=True)
        scale = lax.rsqrt(column / full_width + EPS)
        for j in range(out.shape[2] // 128):
            lo = j * 256
            gate = ins[0][at, lo : lo + 128].astype(F32)
            up = ins[0][at, lo + 128 : lo + 256].astype(F32)
            for s in range(1, SIDE):
                gate = gate + ins[s][at, lo : lo + 128].astype(F32)
                up = up + ins[s][at, lo + 128 : lo + 256].astype(F32)
            gate = gate * scale
            up = up * scale
            out[part, :, j * 128 : (j + 1) * 128] = (gate / (1.0 + jnp.exp(-gate)) * up).astype(BF16)


def hidden_units(blocks, rows, full_width):
    cols = blocks[0].shape[1]
    return pl.pallas_call(
        functools.partial(hidden_kernel, full_width=full_width),
        out_shape=jax.ShapeDtypeStruct((2, rows, cols // 2), BF16),
        in_specs=[VMEM_SPEC] * 4,
        out_specs=VMEM_SPEC,
        cost_estimate=pl.CostEstimate(flops=4_000_000, bytes_accessed=3_000_000, transcendentals=200_000),
        name="hidden_units",
    )(*blocks)


def merge_kernel(at_ref, *refs, chunk):
    ins, out = refs[:4], refs[4]
    plane = SIDE * chunk
    out[plane:, :] = jnp.zeros((out.shape[0] - plane, out.shape[1]), out.dtype)
    for s in range(SIDE):
        at = pl.multiple_of(lax.rem(at_ref[2] - s + SIDE, SIDE) * chunk, chunk)
        out[pl.ds(at, chunk), :] = ins[s][:chunk, :]
        out[plane : plane + 16, pl.ds(at, chunk)] = ins[s][chunk : chunk + 16, :chunk]


def merge_z(at, blocks, chunk):
    return pl.pallas_call(
        functools.partial(merge_kernel, chunk=chunk),
        out_shape=jax.ShapeDtypeStruct((SIDE * chunk + 32, blocks[0].shape[1]), BF16),
        in_specs=[SMEM_SPEC] + [VMEM_SPEC] * 4,
        out_specs=VMEM_SPEC,
        cost_estimate=pl.CostEstimate(flops=0, bytes_accessed=1_200_000, transcendentals=0),
        name="merge_z",
    )(at, *blocks)


def expand_kernel(at_ref, *refs, rows, chunk, turn):
    acts, weights, outs, stage = refs[:8], refs[8:12], refs[12:16], refs[16]
    for part in range(2):

        def body(nb, carry):
            cols = pl.ds(pl.multiple_of(nb * 256, 256), 256)
            acc = None
            for s in range(SIDE):
                term = jnp.dot(
                    acts[part * SIDE + s][:rows, :], weights[s][:, cols], preferred_element_type=F32
                )
                acc = term if acc is None else acc + term
            stage[:, cols] = acc.astype(BF16)
            return carry

        lax.fori_loop(0, stage.shape[1] // 256, body, 0)
        for s in range(SIDE):
            at = pl.multiple_of(lax.rem(at_ref[turn] + s, SIDE) * chunk, chunk)
            outs[s][part * chunk : (part + 1) * chunk, :] = stage[pl.ds(at, chunk), :]
            terms = acts[part * SIDE][rows : rows + 16, pl.ds(at, chunk)].astype(F32)
            for t in range(1, SIDE):
                terms = terms + acts[part * SIDE + t][rows : rows + 16, pl.ds(at, chunk)].astype(F32)
            if part == 0:
                outs[s][2 * chunk :, :] = jnp.zeros((16, stage.shape[1]), BF16)
            outs[s][2 * chunk :, part * chunk : (part + 1) * chunk] = term_rows(
                jnp.sum(terms, axis=0, keepdims=True)
            )


def expand(at, own, other, weights, rows, chunk, turn):
    cols = weights[0].shape[1]
    return pl.pallas_call(
        functools.partial(expand_kernel, rows=rows, chunk=chunk, turn=turn),
        out_shape=[jax.ShapeDtypeStruct((2 * chunk + 16, cols), BF16)] * 4,
        in_specs=[SMEM_SPEC] + [VMEM_SPEC] * 12,
        out_specs=[VMEM_SPEC] * 4,
        scratch_shapes=[pltpu.VMEM((rows, cols), BF16)],
        compiler_params=pltpu.CompilerParams(vmem_limit_bytes=32 << 20),
        cost_estimate=pl.CostEstimate(flops=4 * rows * 2048 * cols, bytes_accessed=10_000_000, transcendentals=0),
        name="gate_up",
    )(at, *own, *other, *weights)


def collect_kernel(page_ref, kv_ref, out_ref):
    def body(i, carry):
        out_ref[i] = kv_ref[page_ref[i]]
        return carry

    lax.fori_loop(0, out_ref.shape[0], body, 0)


def collect(pages, kv):
    count = pages.shape[0]
    return pl.pallas_call(
        collect_kernel,
        out_shape=jax.ShapeDtypeStruct((count,) + kv.shape[1:], kv.dtype),
        in_specs=[SMEM_SPEC, VMEM_SPEC],
        out_specs=VMEM_SPEC,
        compiler_params=pltpu.CompilerParams(vmem_limit_bytes=16 << 20),
        cost_estimate=pl.CostEstimate(flops=0, bytes_accessed=4_000_000, transcendentals=0),
        name="collect_pages",
    )(pages, kv)


def settle_kernel(slot_ref, kv_ref, got_ref, out_ref):
    slots = out_ref.shape[0]

    def keep(i, carry):
        out_ref[i] = kv_ref[i]
        return carry

    lax.fori_loop(0, slots, keep, 0)

    def move(i, carry):
        slot = slot_ref[i]

        @pl.when(slot < slots)
        def _():
            out_ref[slot] = got_ref[i]

        return carry

    lax.fori_loop(0, got_ref.shape[0], move, 0)


def settle(slots, kv, got):
    return pl.pallas_call(
        settle_kernel,
        out_shape=jax.ShapeDtypeStruct(kv.shape, kv.dtype),
        in_specs=[SMEM_SPEC, VMEM_SPEC, VMEM_SPEC],
        out_specs=VMEM_SPEC,
        compiler_params=pltpu.CompilerParams(vmem_limit_bytes=24 << 20),
        cost_estimate=pl.CostEstimate(flops=0, bytes_accessed=12_000_000, transcendentals=0),
        name="settle_pages",
    )(slots, kv, got)


def down(ha, hb, w_down, y, x, na, nb):
    total = None
    for s in range(SIDE):
        wa = lax.dynamic_slice_in_dim(w_down, ((y - s) % SIDE) * na, na, 0)
        term = jnp.dot(ha[s], wa, preferred_element_type=F32)
        total = term if total is None else total + term
    for s in range(SIDE):
        wb = lax.dynamic_slice_in_dim(w_down, SIDE * na + ((x - s) % SIDE) * nb, nb, 0)
        total = total + jnp.dot(hb[s], wb, preferred_element_type=F32)
    return total


def per_device(
    inputs,
    attn_gain,
    query_key_value_weight,
    key_value_pages,
    w_out,
    ffn_gain,
    w_gate_up,
    w_down,
    owner_pool_device,
    context_page_count,
    request_page_slots,
    mig_page,
    mig_dest,
    mig_slot,
):
    y, x, z, c = (lax.axis_index(a) for a in ("y", "x", "z", "c"))
    pool_count = SIDE * SIDE
    here = y * SIDE + x
    total_req, width = inputs.shape
    per_block = total_req // pool_count
    full_width = width * pool_count
    local_slots, page_len = key_value_pages.shape[:2]
    dim = key_value_pages.shape[3] // 2
    qkv_cols = query_key_value_weight.shape[1]
    heads = qkv_cols // dim
    groups = heads - 2
    capacity = max(2, (2 * per_block + pool_count - 1) // pool_count)
    kv = key_value_pages.reshape(local_slots, page_len, 2 * dim)

    block_owner = owner_pool_device.reshape(pool_count, per_block)
    pool_iota = jnp.arange(pool_count, dtype=jnp.int32)
    slot_iota = jnp.arange(capacity, dtype=jnp.int32)
    row_iota = jnp.arange(per_block, dtype=jnp.int32)
    mine = (block_owner == here).astype(jnp.int32)
    mine_rank = jnp.cumsum(mine, axis=1) - 1
    mine_hit = (mine[:, :, None] > 0) & (mine_rank[:, :, None] == slot_iota)
    req_number = pool_iota[:, None] * per_block + row_iota[None, :]
    ids = jnp.where(
        jnp.any(mine_hit, axis=1), jnp.sum(jnp.where(mine_hit, req_number[:, :, None], 0), axis=1), total_req
    ).reshape(-1)
    my_owner = pick(block_owner, here)
    owner_hot = (my_owner[:, None] == pool_iota).astype(jnp.int32)
    my_rank = jnp.sum(jnp.cumsum(owner_hot, axis=0) * owner_hot, axis=1) - 1
    my_place = my_owner * capacity + my_rank
    spread = (jnp.arange(pool_count * capacity, dtype=jnp.int32)[:, None] == my_place[None, :]).astype(BF16)

    move_pages, move_dest, move_slot = mig_page[0], mig_dest[0], mig_slot[0]
    dest_hot = (move_dest[:, None] == pool_iota[None, :]).astype(jnp.int32)
    move_rank = jnp.sum(jnp.cumsum(dest_hot, axis=0) * dest_hot, axis=1) - 1
    cap_iota = jnp.arange(MCAP, dtype=jnp.int32)
    move_hits = (move_dest[:, None, None] == pool_iota[None, :, None]) & (
        move_rank[:, None, None] == cap_iota[None, None, :]
    )
    move_filled = jnp.any(move_hits, axis=0)
    page_index = jnp.sum(jnp.where(move_hits, move_pages[:, None, None], 0), axis=0).reshape(-1)
    send_slots = jnp.where(
        move_filled, jnp.sum(jnp.where(move_hits, move_slot[:, None, None], 0), axis=0), local_slots
    )

    at = jnp.stack([y, x, z, c]).astype(jnp.int32)
    product = qkv_product(inputs, attn_gain, query_key_value_weight)
    at_first, page_index, product = lax.optimization_barrier((at, page_index, product))
    summands = lax.all_to_all(
        product.reshape(pool_count, per_block, qkv_cols + 128), POOL, split_axis=0, concat_axis=0, tiled=True
    )

    def exchange(blocks, axis):
        got = {s: shift(blocks[s], axis, s) for s in (2, 1, 3)}
        return [blocks[0], got[1], got[2], got[3]]

    hidden_local = w_gate_up.shape[2]
    unit_a = 512
    unit_b = hidden_local // SIDE - unit_a
    my_lengths = lax.dynamic_slice_in_dim(context_page_count, here * per_block, per_block)
    half = dim // 2
    frequency = jnp.exp(jnp.arange(half, dtype=F32) * (-2.0 * math.log(500000.0) / dim))
    angles = (my_lengths * page_len).astype(F32)[:, None] * frequency[None, :]
    cosine, sine = jnp.cos(angles), jnp.sin(angles)
    send_rows = ready_rows(
        spread,
        jnp.concatenate([cosine, cosine], axis=1),
        jnp.concatenate([-sine, sine], axis=1),
        summands,
        dim,
        full_width,
    )
    send_wa, send_wb = regroup(at_first, w_gate_up, unit_a, unit_b)
    send_pages = collect(page_index, kv)
    send_wa, send_wb, send_pages, send_rows = lax.optimization_barrier((send_wa, send_wb, send_pages, send_rows))
    slot_lanes = jnp.pad(
        jnp.broadcast_to(send_slots.astype(BF16)[:, None, :], (pool_count, capacity, MCAP)),
        ((0, 0), (0, 0), (0, 128 - MCAP)),
    )
    rows_all = lax.all_to_all(
        jnp.concatenate([send_rows.reshape(pool_count, capacity, qkv_cols), slot_lanes], axis=2),
        POOL,
        split_axis=0,
        concat_axis=0,
        tiled=True,
    )
    got_slots = rows_all[:, 0, qkv_cols : qkv_cols + MCAP].astype(jnp.int32).reshape(-1)
    attn_rows = rows_all[:, :, :qkv_cols]
    wa, wb = [send_wa[0]] + [None] * 3, [send_wb[0]] + [None] * 3
    wa[2] = shift(send_wa[2], "y", 2)
    wb[2] = shift(send_wb[2], "x", 2)
    wa[1] = shift(send_wa[1], "y", 1)
    wb[1] = shift(send_wb[1], "x", 1)
    wa[3] = shift(send_wa[3], "y", 3)

    attn = attend(ids, context_page_count, request_page_slots.T, attn_rows.reshape(-1, heads, dim), kv)
    late_b, attn = lax.optimization_barrier((send_wb[3], attn))
    wb[3] = shift(late_b, "x", 3)
    returned = lax.all_to_all(
        attn.reshape(pool_count, capacity, groups * dim), POOL, split_axis=0, concat_axis=0, tiled=True
    ).reshape(pool_count * capacity, groups * dim)
    *early, returned = lax.optimization_barrier((wa[2], wb[2], wa[1], wb[1], wa[3], returned))
    wa[2], wb[2], wa[1], wb[1], wa[3] = early
    my_rows = jnp.dot(spread.T, returned, preferred_element_type=F32).astype(BF16)

    hcols = groups * dim // 2
    col_a = place(gather_direct(my_rows[:, :hcols], "x"), x)
    col_b = place(gather_direct(my_rows[:, hcols:], "y"), y)
    full_a = place(gather_direct(col_a, "y"), y).reshape(total_req, hcols)
    full_b = place(gather_direct(col_b, "x"), x).transpose(1, 0, 2, 3).reshape(total_req, hcols)
    partial = jnp.dot(full_a, w_out[:hcols], preferred_element_type=F32) + jnp.dot(
        full_b, w_out[hcols:], preferred_element_type=F32
    )

    wb[3], send_pages, partial = lax.optimization_barrier((wb[3], send_pages, partial))
    got_pages = lax.all_to_all(
        send_pages.reshape(pool_count, MCAP, page_len, 2 * dim),
        POOL,
        split_axis=0,
        concat_axis=0,
        tiled=True,
    )

    chunk = total_req // 8
    by_core = partial.reshape(SIDE, 2, chunk, width)
    mixed = pick(by_core, c, 1) + swap(pick(by_core, 1 - c, 1).astype(BF16)).astype(F32)
    mixed = mixed.astype(BF16)
    mid = reduce_four(lambda k: pick(mixed, k), "z", z) + lax.dynamic_slice_in_dim(
        inputs, (z * 2 + c) * chunk, chunk
    ).astype(F32)
    mid_sq = jnp.sum(mid * mid, axis=1)
    ffn_rows = (mid * ffn_gain.astype(F32)).astype(BF16)

    sq_row = jnp.pad(jnp.stack(three_parts(mid_sq), axis=0), ((0, 13), (0, width - chunk))).astype(BF16)
    plane = SIDE * chunk
    block = merge_z(at, gather_direct(jnp.concatenate([ffn_rows, sq_row], axis=0), "z"), chunk)

    got_pages, block = lax.optimization_barrier((got_pages, block))

    def join(b):
        return jnp.concatenate(b, axis=0) if isinstance(b, tuple) else b

    own_y = [join(b) for b in gather_ring(block, "y")]
    own_x = [join(b) for b in gather_ring(block, "x")]
    oth_0 = swap(block)
    oth_y = [oth_0] + [swap(b) for b in own_y[1:]]
    oth_x = [oth_0] + [swap(b) for b in own_x[1:]]

    prod_a = expand(at, own_y, oth_y, wa, plane, chunk, 1)
    prod_b = expand(at, own_x, oth_x, wb, plane, chunk, 0)
    hid_a = hidden_units(exchange(prod_a, "x"), chunk, full_width)
    hid_b = hidden_units(exchange(prod_b, "y"), chunk, full_width)

    rows_ha = place(gather_direct(hid_a, "x"), x).reshape(total_req, unit_a)
    rows_hb = place(gather_direct(hid_b, "y"), y).reshape(total_req, unit_b)
    got_pages, rows_ha = lax.optimization_barrier((got_pages, rows_ha))
    all_ha = [join(b) for b in gather_ring(rows_ha, "y")]
    all_hb = [join(b) for b in gather_ring(rows_hb, "x")]
    new_pool = settle(got_slots, kv, got_pages.reshape(-1, page_len, 2 * dim))
    new_pool, all_ha[2] = lax.optimization_barrier((new_pool, all_ha[2]))
    down_part = down(all_ha, all_hb, w_down, y, x, unit_a, unit_b).reshape(SIDE, 2, chunk, width)
    low = (down_part[:, 0] + swap(down_part[:, 1].astype(BF16)).astype(F32)).astype(BF16)
    out_rows = (reduce_four(lambda k: pick(low, k), "z", z) + mid).astype(BF16)
    out_own = place(gather_direct(out_rows, "z"), z)
    out_oth = swap(out_own)
    first = c == 0
    out = jnp.stack(
        [jnp.where(first, out_own, out_oth), jnp.where(first, out_oth, out_own)], axis=1
    ).reshape(total_req, width)

    return (out, new_pool.reshape(key_value_pages.shape))


def solution(mesh):
    grid = Mesh(mesh.devices.reshape(SIDE, SIDE, SIDE, 2), ("y", "x", "z", "c"))
    tensor = ("z", "c")
    return jax.shard_map(
        per_device,
        mesh=grid,
        in_specs=(
            P(None, POOL),
            P(POOL),
            P(POOL, tensor),
            P(POOL, None, tensor, None),
            P(tensor, POOL),
            P(POOL),
            P(POOL, None, tensor),
            P(tensor, POOL),
            P(),
            P(),
            P(),
            P(POOL, None),
            P(POOL, None),
            P(POOL, None),
        ),
        out_specs=(P(None, POOL), P(POOL, None, tensor, None)),
        check_vma=False,
    )
```
